256 devices in a mesh: dp: 16 (over z, core), seq: 16 (over x, y).
Axes of the slice: x: 4, y: 4, z: 8, core: 2. Of those that a mesh axis runs over, the one named last changes fastest.
Arguments:
- queries: bfloat16 [32768, 4096], P(('dp', 'seq')), may hold values from -6 to 6
- key_heads: bfloat16 [32768, 512], P(('dp', 'seq')), may hold values from -6 to 6
- value_heads: bfloat16 [32768, 512], P(('dp', 'seq')), may hold values from -6 to 6
- upper_cotangent: bfloat16 [32768, 4096], P(('dp', 'seq')), may hold values from -1.5 to 1.5
- readout: bfloat16 [32, 128], replicated, may hold values from -0.09375 to 0.09375
- base_value: float32 [32768], P(('dp', 'seq')), may hold values from -4 to 4
- old_values: float32 [32768], P(('dp', 'seq')), may hold values from -5 to 5
- returns: float32 [32768], P(('dp', 'seq')), may hold values from -6 to 6
- source_index: int32 [16, 2048], P('dp'), may hold values from 0 to 2047, as said below
- doc_lengths: int32 [16, 4], P('dp'), may hold values from 1 to 1024, 2048 in all within a row
Outputs:
- values: float32 [32768], P(('dp', 'seq'))
- grad_queries: bfloat16 [32768, 4096], P(('dp', 'seq'))
- grad_key_heads: bfloat16 [32768, 512], P(('dp', 'seq'))
- grad_value_heads: bfloat16 [32768, 512], P(('dp', 'seq'))
- grad_readout: float32 [32, 128], P('seq', 'dp')
The draws below stay inside these ranges and needn't reach their ends.
Inputs may be any that keep to these rules, and one draw needn't show every extreme that they name: `source_index`: each row is a permutation of its positions. Of the 128 trainer positions of one seq index, at most 16 take their generator position from the 128 positions of any one seq index, and in every row each seq index reaches 16 with one source; every seq index receives and sends the same multiset of such counts.
All inputs are finite; a program needn't handle non-finite values.
Results may differ from the reference program's by a relative error of at most 0.012.
The reference program's roundings to bfloat16 on the way count: a program that leaves them out, or rounds other values in their place, can miss the bound.
Values may be sent and summed in bfloat16 or wider, within the bound.
A program may use at most 64 MiB of HBM per device.

```python
import math
import jax
import jax.numpy as jnp
import numpy as np
from jax import lax

H = 32
KVH = 4
HD = 128
T_DEV = 128
DA = 4096
KVD = 512
L = 2048
TOKENS = 32768
DOCS = 4
MAXDOC = 1024
N_DP = 16
N_SEQ = 16


def source_table(key):
    length = T_DEV * N_SEQ
    capacity = 2 * T_DEV // N_SEQ

    def one_row(row_key):
        split_keys = jax.random.split(row_key, 5)
        chosen = jax.random.permutation(split_keys[0], (N_SEQ - 1) * capacity)[:T_DEV - capacity]
        others = jnp.sum(chosen[:, None] // capacity == jnp.arange(N_SEQ - 1, dtype=jnp.int32)[None, :], axis=0).astype(jnp.int32)
        amounts = jnp.concatenate([jnp.full((1,), capacity, jnp.int32), others])
        row_order = jax.random.permutation(split_keys[1], N_SEQ)
        column_order = jax.random.permutation(split_keys[2], N_SEQ)
        counts = amounts[(row_order[:, None] + column_order[None, :]) % N_SEQ]
        labels = jax.vmap(lambda amount: jnp.repeat(jnp.arange(N_SEQ, dtype=jnp.int32), amount, total_repeat_length=T_DEV))(counts)
        labels = jax.vmap(jax.random.permutation)(jax.random.split(split_keys[3], N_SEQ), labels).reshape(length)
        one_hot = (labels[:, None] == jnp.arange(N_SEQ, dtype=jnp.int32)[None, :]).astype(jnp.int32)
        ranking = jnp.sum((jnp.cumsum(one_hot, axis=0) - 1) * one_hot, axis=1)
        shuffles = jax.vmap(lambda sub_key: jax.random.permutation(sub_key, T_DEV))(jax.random.split(split_keys[4], N_SEQ))
        within = shuffles[labels, ranking]
        return (labels * T_DEV + within).astype(jnp.int32)
    row_keys = jax.vmap(lambda row_number: jax.random.fold_in(jax.random.fold_in(key, 71), row_number))(jnp.arange(N_DP, dtype=jnp.int32))
    return jax.vmap(one_row)(row_keys)


def draw_source_index(key, part):
    return source_table(key)


def base_draw(key):
    own_key = jax.random.fold_in(key, 23)
    return jnp.clip(jax.random.normal(own_key, (TOKENS,), jnp.float32), -4.0, 4.0)


def draw_base_value(key, part):
    return base_draw(key)


def draw_old_values(key, part):
    length = T_DEV * N_SEQ
    noise = jnp.clip(jax.random.normal(jax.random.fold_in(key, 29), (TOKENS,), jnp.float32), -4.0, 4.0)
    trainer = base_draw(key) + 0.25 * noise
    sources = source_table(key)
    offsets = (jnp.arange(N_DP, dtype=jnp.int32) * length)[:, None]
    flat_index = (sources + offsets).reshape(TOKENS)
    return jnp.zeros((TOKENS,), jnp.float32).at[flat_index].set(trainer)


def draw_queries(key, part):
    own_key = jax.random.fold_in(key, 61)
    drawn = jnp.clip(jax.random.normal(own_key, (TOKENS, H, HD), jnp.float32), -6.0, 6.0)
    return drawn.reshape(TOKENS, H * HD).astype(jnp.bfloat16)


def draw_key_heads(key, part):
    own_key = jax.random.fold_in(key, 67)
    drawn = jnp.clip(jax.random.normal(own_key, (TOKENS, KVH, HD), jnp.float32), -6.0, 6.0)
    return drawn.reshape(TOKENS, KVH * HD).astype(jnp.bfloat16)


def block_levels(rng, dims, cuts, low, top_value):
    def one(axis_at, parts):
        heights = jax.random.uniform(jax.random.fold_in(jax.random.fold_in(rng, 6), axis_at), (parts,), jnp.float32, low / len(cuts), top_value / len(cuts))
        return jnp.repeat(jnp.exp(heights), dims[axis_at] // parts).reshape((-1,) + (1,) * (len(dims) - axis_at - 1))

    level = one(*cuts[0])
    for cut in cuts[1:]:
        level = level * one(*cut)
    return level


def length_profile(count, total, bound, lean):
    portions = [(1 << 20) // math.isqrt(standing ** lean) + 1 for standing in range(2, count + 1)]
    spare, holding = total - bound - (count - 1), [1] * (count - 1)
    while spare > 0:
        movable = [i for i in range(count - 1) if holding[i] < bound]
        mass, remaining = sum([portions[i] for i in movable]), spare
        for i in movable:
            extra = min(bound - holding[i], max(1, remaining * portions[i] // mass), spare)
            holding[i] = holding[i] + extra
            spare = spare - extra
    return np.array([bound] + holding)


def uneven(rng, count, total, bound, slope):
    if count == 2:
        one = jax.random.randint(rng, (), max(1, total - bound), min(bound, total - 1) + 1)
        return jnp.stack([one, total - one])
    tallies = jnp.asarray(length_profile(count, total, bound, slope), jnp.int32)
    pairs = (count - 1) // 2
    source_of, taker = tallies[1:1 + 2 * pairs:2], tallies[2:2 + 2 * pairs:2]
    room = jnp.minimum(source_of - 1, bound - taker)
    passed = jax.random.randint(jax.random.fold_in(rng, 1), (pairs,), 0, 1 << 20) % (room + 1)
    tallies = tallies.at[1:1 + 2 * pairs:2].set(source_of - passed).at[2:2 + 2 * pairs:2].set(taker + passed)
    return tallies[jax.random.permutation(jax.random.fold_in(rng, 2), count)]


def scatter_about(key, dims, width, reach, shards=(), held_as=jnp.bfloat16):
    values = jax.random.normal(key, dims, jnp.float32) * width
    if len(shards) > 0:
        values = block_levels(key, dims, shards, -0.22, 0.18) * values
    return jnp.clip(values, min=-reach, max=reach).astype(held_as)


def setup_inputs(seed: int = 0) -> dict:
    seeds = jax.random.split(jax.random.key(seed), 11)
    queries = draw_queries(jax.random.fold_in(seeds[10], 71), 0)
    key_heads = draw_key_heads(jax.random.fold_in(seeds[10], 71), 0)
    value_heads = scatter_about(seeds[2], (TOKENS, KVD), 1.0, 6.0, ((0, 256),))
    upper_cotangent = scatter_about(seeds[3], (TOKENS, DA), 0.25, 1.5, ((0, 256),))
    readout = scatter_about(seeds[4], (H, HD), (H * HD) ** -0.5, 0.09375)
    base_value = draw_base_value(jax.random.fold_in(seeds[10], 71), 0)
    old_values = draw_old_values(jax.random.fold_in(seeds[10], 71), 0)
    returns = scatter_about(seeds[7], (TOKENS,), 1.0, 6.0, ((0, 256),), jnp.float32)
    source_index = draw_source_index(jax.random.fold_in(seeds[10], 71), 0)
    doc_lengths = jax.vmap(lambda own: uneven(own, DOCS, L, MAXDOC, 2))(jax.random.split(seeds[9], N_DP)).reshape((N_DP, DOCS)).astype(jnp.int32)
    return dict(queries=queries, key_heads=key_heads, value_heads=value_heads, upper_cotangent=upper_cotangent, readout=readout, base_value=base_value, old_values=old_values, returns=returns, source_index=source_index, doc_lengths=doc_lengths)


clip_range = 0.2
smooth_width = 0.1
loss_scale = 16.0

def doc_starts(doc_sizes, length):
    doc_ends = jnp.cumsum(doc_sizes).astype(jnp.int32)
    doc_firsts = (doc_ends - doc_sizes).astype(jnp.int32)
    positions = jnp.arange(length, dtype=jnp.int32)
    inside = (positions[:, None] >= doc_firsts[None, :]) & (positions[:, None] < doc_ends[None, :])
    return lax.optimization_barrier(jnp.sum(jnp.where(inside, doc_firsts[None, :], 0), axis=1)).astype(jnp.int32)

def value_grad(values, old_now, return_now):
    ratio = jnp.tanh((values - old_now) / clip_range)
    clipped = old_now + clip_range * ratio
    plain_gap = values - return_now
    clip_gap = clipped - return_now
    mixing = jax.nn.sigmoid((plain_gap * plain_gap - clip_gap * clip_gap) / smooth_width)
    return loss_scale * (mixing * plain_gap + (1.0 - mixing) * clip_gap * (1.0 - ratio * ratio))

def rounded(array):
    return lax.optimization_barrier(array.astype(jnp.bfloat16)).astype(jnp.float32)

def reference(queries, key_heads, value_heads, upper_cotangent, readout, base_value, old_values, returns, source_index, doc_lengths):
    length = T_DEV * N_SEQ
    group = H // KVH
    share_heads = min(group, H // N_SEQ)
    score_scale = HD ** (-0.5)
    read_grid = readout.astype(jnp.float32).reshape(KVH, group, HD)

    def block_sum(each):
        partial_sums = rounded(lax.optimization_barrier(jnp.sum(each.reshape(group // share_heads, share_heads, length, HD), axis=1)))
        return lax.optimization_barrier(jnp.sum(partial_sums, axis=0)).astype(jnp.bfloat16)

    def per_row(row_args):
        query_row, key_row, value_row, upper_row, base_row, old_row, return_row, source_row, size_row = row_args
        starts = doc_starts(size_row, length)
        positions = jnp.arange(length, dtype=jnp.int32)
        visible = (starts[:, None] == starts[None, :]) & (positions[None, :] <= positions[:, None])

        def forward_group(group_args):
            query_group, key_one, value_one = group_args
            scores = jnp.einsum('qah,kh->aqk', query_group.astype(jnp.float32), key_one.astype(jnp.float32)) * score_scale
            masked = jnp.where(visible[None], scores, -1e+30)
            row_max = lax.optimization_barrier(jnp.max(masked, axis=2, keepdims=True))
            row_total = lax.optimization_barrier(jnp.sum(jnp.where(visible[None], jnp.exp(masked - row_max), 0.0), axis=2, keepdims=True))
            log_total = row_max + jnp.log(row_total)
            weights = rounded(jnp.where(visible[None], jnp.exp(masked - log_total), 0.0))
            attn_out = jnp.einsum('aqk,kh->qah', weights, value_one.astype(jnp.float32)).astype(jnp.bfloat16)
            return (attn_out, log_total[:, :, 0])
        attn_out, log_total = lax.map(forward_group, (query_row.transpose(1, 0, 2, 3), key_row.transpose(1, 0, 2), value_row.transpose(1, 0, 2)))
        attn_out = attn_out.transpose(1, 0, 2, 3)
        out_float = attn_out.astype(jnp.float32)
        values = base_row + jnp.einsum('qcah,cah->q', out_float, read_grid)
        old_now = jnp.take(old_row, source_row)
        return_now = jnp.take(return_row, source_row)
        value_cot = value_grad(values, old_now, return_now)
        out_cot = (upper_row.astype(jnp.float32) + value_cot[:, None, None, None] * read_grid[None]).astype(jnp.bfloat16)
        deltas = lax.optimization_barrier(jnp.sum(out_cot.astype(jnp.float32) * out_float, axis=3))
        readout_part = jnp.einsum('q,qcah->cah', value_cot, out_float)

        def backward_group(group_args):
            query_group, key_one, value_one, cot_group, log_group, delta_group = group_args
            query_float = query_group.astype(jnp.float32)
            key_float = key_one.astype(jnp.float32)
            cot_float = cot_group.astype(jnp.float32)
            scores = jnp.einsum('qah,kh->aqk', query_float, key_float) * score_scale
            masked = jnp.where(visible[None], scores, -1e+30)
            weights = jnp.where(visible[None], jnp.exp(masked - log_group[:, :, None]), 0.0)
            grad_weights = jnp.einsum('qah,kh->aqk', cot_float, value_one.astype(jnp.float32))
            grad_scores = rounded(weights * (grad_weights - delta_group.T[:, :, None]) * score_scale)
            grad_query = jnp.einsum('aqk,kh->qah', grad_scores, key_float).astype(jnp.bfloat16)
            key_each = jnp.einsum('aqk,qah->akh', grad_scores, query_float)
            value_each = jnp.einsum('aqk,qah->akh', rounded(weights), cot_float)
            return (grad_query, block_sum(key_each), block_sum(value_each))
        grad_query, grad_key, grad_value = lax.map(backward_group, (query_row.transpose(1, 0, 2, 3), key_row.transpose(1, 0, 2), value_row.transpose(1, 0, 2), out_cot.transpose(1, 0, 2, 3), log_total, deltas.transpose(1, 0, 2)))
        grad_query = grad_query.transpose(1, 0, 2, 3).reshape(length, H * HD)
        grad_key = grad_key.transpose(1, 0, 2).reshape(length, KVH * HD)
        grad_value = grad_value.transpose(1, 0, 2).reshape(length, KVH * HD)
        return (values, grad_query, grad_key, grad_value, readout_part)
    row_inputs = (queries.reshape(N_DP, length, KVH, group, HD), key_heads.reshape(N_DP, length, KVH, HD), value_heads.reshape(N_DP, length, KVH, HD), upper_cotangent.reshape(N_DP, length, KVH, group, HD), base_value.reshape(N_DP, length), old_values.reshape(N_DP, length), returns.reshape(N_DP, length), source_index, doc_lengths)
    values, grad_queries, grad_keys, grad_values, readout_parts = lax.map(per_row, row_inputs)
    return (values.reshape(N_DP * length), grad_queries.reshape(N_DP * length, H * HD), grad_keys.reshape(N_DP * length, KVH * HD), grad_values.reshape(N_DP * length, KVH * HD), lax.optimization_barrier(jnp.sum(readout_parts, axis=0)).reshape(H, HD))
```

```python
import jax
import jax.numpy as jnp
from jax import lax
from jax.experimental import pallas as pl
from jax.experimental.pallas import tpu as pltpu
from jax.sharding import PartitionSpec as P

T = 128
HD = 128
NH = 32
GROUP = 8
NKV = 4
SEQ = 16
DP = 16
NS = 9
ROWS = GROUP * T
CHUNKS = ((0, 256), (256, 512), (512, 768), (768, 1024), (1024, 1152))
KEPT = {0: 0, 2: 1, 4: 2, 8: 3}
SCALE = HD ** (-0.5)
LOG2E = 1.4426950408889634
MESH = pl.DeviceIdType.MESH
F32 = jnp.float32
BF16 = jnp.bfloat16
NT = (((1,), (1,)), ((), ()))
TN = (((0,), (0,)), ((), ()))


def dot(a, b, dims=(((1,), (0,)), ((), ()))):
    return lax.dot_general(a, b, dims, preferred_element_type=F32)


def heads_of(ref, first, count):
    wide = ref[:, pl.ds(pl.multiple_of(first * HD, HD), count * HD)]
    return jnp.concatenate([wide[:, a * HD : (a + 1) * HD] for a in range(count)], axis=0)


def kernel(
    q_ref, k_ref, v_ref, u_ref, ro_ref, base_ref, old_ref, ret_ref, src_ref, len_ref,
    vals_ref, dq_ref, dk_ref, dv_ref, gr_ref,
    kv, p_sc, t_sc, out_sc, dol_sc, rl_sc, dl_sc, bias, vacc, cot_sc, ro, og, sb, rb, acc, gs, g1, g2, gx, tmp,
    kv_send, kv_recv, tmp_recv, og_send, og_recv, sb_send, rb_recv, g_send, g_recv, h_send, h_recv,
):
    me = lax.axis_index("seq")
    my_dp = lax.axis_index("dp")
    x, y = me // 4, lax.rem(me, 4)

    def seq_peer(number):
        return {"seq": number}

    def row_peer(step):
        return x * 4 + lax.rem(y + step, 4)

    def x_peer(step):
        return lax.rem(x + step, 4) * 4 + y

    def send(src, dst, send_sem, recv_sem, peer):
        return pltpu.make_async_remote_copy(
            src_ref=src, dst_ref=dst, send_sem=send_sem, recv_sem=recv_sem, device_id=peer, device_id_type=MESH
        )

    def kv_copy(src, dst, half, peer, number):
        return send(
            kv.at[src, half], kv.at[dst, half], kv_send.at[number, half], kv_recv.at[dst, half], seq_peer(peer)
        )

    barrier = pltpu.get_barrier_semaphore()
    for step in range(1, SEQ):
        pl.semaphore_signal(
            barrier, inc=1, device_id={"seq": lax.rem(me + step, SEQ)}, device_id_type=MESH
        )
    for step in range(1, DP):
        pl.semaphore_signal(
            barrier, inc=1, device_id={"dp": lax.rem(my_dp + step, DP)}, device_id_type=MESH
        )

    ro[...] = ro_ref[...].astype(F32)
    for c in range(NKV):
        kv[c, 0, 0:T, :] = k_ref[:, c * HD : (c + 1) * HD]
        kv[c, 1, 0:T, :] = v_ref[:, c * HD : (c + 1) * HD]
    og[me] = jnp.concatenate([old_ref[...], ret_ref[...], jnp.zeros((6, T), F32)], axis=0)

    wraps = [y + step >= 4 for step in range(4)]
    lifts = [4 * (y + step >= 4).astype(jnp.int32) for step in range(4)]

    def piece(c, slot):
        return kv.at[c, :, pl.ds(pl.multiple_of(slot * T, T), T), :]

    def kv_copy(c, src, dst, peer, number):
        return send(
            piece(c, src), piece(c, dst), kv_send.at[c, number], kv_recv.at[c, dst], seq_peer(peer)
        )

    def landed(c, slot):
        kv_copy(c, 0, slot, 0, 0).wait_recv()

    pl.semaphore_wait(barrier, SEQ + DP - 2)

    def tmp_copy(c):
        return send(piece(c, 0), tmp.at[c], kv_send.at[c, 1], tmp_recv.at[c], seq_peer(x_peer(3)))

    def tmp_forward(c):
        return send(
            tmp.at[c], piece(c, 8), kv_send.at[c, 8], kv_recv.at[c, 8], seq_peer(x_peer(3))
        )

    def gather_start(c):
        kv_copy(c, 0, 4, x_peer(1), 0).start()
        tmp_copy(c).start()
        for step in range(1, 4):

            @pl.when(jnp.logical_not(wraps[step]))
            def _():
                kv_copy(c, 0, step, row_peer(step), 1 + step).start()

    def gather_forward(c):
        landed(c, 4)
        for step in (1, 3, 2):

            @pl.when(wraps[step])
            def _():
                kv_copy(c, 4, step, row_peer(step), 1 + step).start()

            if step != 2:

                @pl.when(jnp.logical_not(wraps[step]))
                def _():
                    kv_copy(c, 4, step + 4, row_peer(step), 4 + step).start()

        tmp_copy(c).wait_recv()
        tmp_forward(c).start()

    def gather_more(c):
        landed(c, 2)
        kv_copy(c, 2, 6, x_peer(1), 6).start()
        landed(c, 8)
        for step in (1, 3):

            @pl.when(wraps[step])
            def _():
                kv_copy(c, 8, step + 4, row_peer(step), 4 + step).start()

    for c in range(NKV):
        gather_start(c)

    def og_copy(step):
        return send(
            og.at[me], og.at[me], og_send.at[step], og_recv.at[step], seq_peer(lax.rem(me + step, SEQ))
        )

    for step in range(1, SEQ):
        og_copy(step).start()

    own_first = me * T
    place = own_first + lax.broadcasted_iota(jnp.int32, (T, 1), 0)
    c1 = len_ref[0, 0]
    c2 = c1 + len_ref[0, 1]
    c3 = c2 + len_ref[0, 2]
    first = jnp.where(place >= c3, c3, jnp.where(place >= c2, c2, jnp.where(place >= c1, c1, 0)))
    lane = lax.broadcasted_iota(jnp.int32, (1, T), 1)
    for slot in range(NS):
        key_place = own_first - T * slot + lane
        seen = (key_place >= first) & (key_place <= place)
        bias[:, slot * T : (slot + 1) * T] = jnp.where(seen, 0.0, -1e30)
    sub = lax.broadcasted_iota(jnp.int32, (T, T), 0)
    lanes = lax.broadcasted_iota(jnp.int32, (T, T), 1)
    own_src = src_ref[pl.ds(me, 1), :].astype(F32)
    columns = jnp.where(sub == 0, base_ref[...], jnp.where(sub == 1, own_src, 0.0)).T
    base_col = columns[:, 0:1]
    src_col = columns[:, 1:2]

    vacc[...] = jnp.zeros_like(vacc)
    gather_forward(0)
    gather_forward(1)
    gather_more(0)

    def forward(c, carry):
        @pl.when(c + 2 < NKV)
        def _():
            gather_forward(c + 2)

        @pl.when(c + 1 < NKV)
        def _():
            gather_more(c + 1)

        for slot in (1, 3, 5, 7, 6):
            landed(c, slot)
        h0 = c * GROUP
        q = heads_of(q_ref, h0, GROUP)
        top = None
        for low, high in CHUNKS:
            s = dot(q, kv[c, 0, low:high, :], NT)
            s = s.reshape(GROUP, T, high - low) * (SCALE * LOG2E) + bias[:, low:high][None]
            s = s.reshape(ROWS, high - low)
            t_sc[:, low:high] = s
            for at in range(0, high - low, T):
                part = s[:, at : at + T]
                top = part if top is None else jnp.maximum(top, part)
        top = jnp.max(top, axis=1, keepdims=True)
        total = None
        o = None
        for low, high in CHUNKS:
            e = jnp.exp2(t_sc[:, low:high] - top)
            for at in range(0, high - low, T):
                part = e[:, at : at + T]
                total = part if total is None else total + part
            e = e.astype(BF16)
            p_sc[c, :, low:high] = e
            part = dot(e, kv[c, 1, low:high, :])
            o = part if o is None else o + part
        rl = 1.0 / jnp.sum(total, axis=1, keepdims=True)
        rl_sc[c] = jnp.broadcast_to(rl, (ROWS, HD))
        o = (o * rl).astype(BF16)
        summed = vacc[...]
        for a in range(GROUP):
            one = o[a * T : (a + 1) * T]
            out_sc[:, pl.ds(pl.multiple_of((h0 + a) * HD, HD), HD)] = one
            summed = summed + one.astype(F32) * ro[pl.ds(h0 + a, 1), :]
        vacc[...] = summed
        return carry

    lax.fori_loop(0, NKV, forward, 0)

    for step in range(1, SEQ):
        og_copy(step).wait_recv()
    old_acc = jnp.zeros((T, T), F32)
    ret_acc = jnp.zeros((T, T), F32)
    for block in range(SEQ):
        same = src_col == (lane + block * T).astype(F32)
        old_acc = old_acc + jnp.where(same, og[block, 0:1, :], 0.0)
        ret_acc = ret_acc + jnp.where(same, og[block, 1:2, :], 0.0)
    old_now = jnp.sum(old_acc, axis=1, keepdims=True)
    return_now = jnp.sum(ret_acc, axis=1, keepdims=True)
    values = base_col + jnp.sum(vacc[...], axis=1, keepdims=True)
    vals_ref[...] = jnp.where(lanes == 0, values, 0.0).T[0:1, :]
    ratio = jnp.tanh((values - old_now) / 0.2)
    plain = values - return_now
    gap = old_now + 0.2 * ratio - return_now
    mixing = jax.nn.sigmoid((plain * plain - gap * gap) / 0.1)
    cot = 16.0 * (mixing * plain + (1.0 - mixing) * gap * (1.0 - ratio * ratio))
    cot_sc[...] = jnp.broadcast_to(cot, (T, HD))

    def g_copy(step):
        peer = lax.rem(me + step, SEQ)
        return send(gs.at[peer], g1.at[me], g_send.at[step], g_recv.at[step], seq_peer(peer))

    def h_copy(step):
        peer = lax.rem(my_dp + step, DP)
        return send(gx, g2.at[my_dp], h_send.at[step], h_recv.at[step], {"dp": peer})

    wide_cot = cot_sc[...]
    for h in range(NH):
        o = out_sc[:, h * HD : (h + 1) * HD].astype(F32)
        gs[h // 2, h % 2 : h % 2 + 1, :] = jnp.sum(wide_cot * o, axis=0, keepdims=True)
    g1[me] = gs[me]
    for step in range(1, SEQ):
        g_copy(step).start()

    def rb_copy(c, slot, peer):
        return send(
            sb.at[c, slot], rb.at[c, slot], sb_send.at[c, slot], rb_recv.at[c, slot], seq_peer(peer)
        )

    def came(c, slot):
        rb_copy(c, slot, 0).wait_recv()

    def got(c, slot, half):
        return rb[c, slot, half].astype(F32)

    def backward(c):
        h0 = c * GROUP
        cot = cot_sc[...]
        q = heads_of(q_ref, h0, GROUP)
        dols = []
        dls = []
        for a in range(GROUP):
            cols = pl.ds(pl.multiple_of((h0 + a) * HD, HD), HD)
            row = pl.ds(h0 + a, 1)
            o = out_sc[:, cols].astype(F32)
            g = (u_ref[:, cols].astype(F32) + cot * ro[row, :]).astype(BF16).astype(F32)
            rl = rl_sc[c, a * T : (a + 1) * T, :]
            dls.append(jnp.broadcast_to(jnp.sum(g * o, axis=1, keepdims=True), (T, HD)) * rl)
            dols.append((g * rl).astype(BF16))
        dol = jnp.concatenate(dols, axis=0)
        dl_sc[...] = jnp.concatenate(dls, axis=0)
        dol_sc[...] = dol
        dq = None
        for low, high in CHUNKS:
            dol = dol_sc[...]
            keys = kv[c, 0, low:high, :]
            dl = dl_sc[...]
            if high - low > T:
                dl = jnp.concatenate([dl] * ((high - low) // T), axis=1)
            p = p_sc[c, :, low:high]
            ds = (p.astype(F32) * (dot(dol, kv[c, 1, low:high, :], NT) - dl)).astype(BF16)
            part = dot(ds, keys)
            dq = part if dq is None else dq + part
            dk = dot(ds, q, TN) * SCALE
            dv = dot(p, dol, TN)
            for at in range(0, high - low, T):
                slot = (low + at) // T
                if slot in KEPT:
                    acc[c, KEPT[slot], 0] = dk[at : at + T]
                    acc[c, KEPT[slot], 1] = dv[at : at + T]
                else:
                    sb[c, slot, 0] = dk[at : at + T].astype(BF16)
                    sb[c, slot, 1] = dv[at : at + T].astype(BF16)
        dq = (dq * SCALE).astype(BF16)
        for a in range(GROUP):
            dq_ref[:, pl.ds(pl.multiple_of((h0 + a) * HD, HD), HD)] = dq[a * T : (a + 1) * T]
        rb_copy(c, 6, x_peer(3)).start()
        for slot in (5, 7, 1, 3):
            rb_copy(c, slot, row_peer(4 - slot % 4)).start()

    def second(c):
        came(c, 6)
        for half in range(2):
            sb[c, 2, half] = (acc[c, KEPT[2], half] + got(c, 6, half)).astype(BF16)
        rb_copy(c, 2, row_peer(2)).start()

    def third(c):
        for slot in (5, 7, 1, 3, 2):
            came(c, slot)
        for half in range(2):
            r5, r7 = got(c, 5, half), got(c, 7, half)
            s8 = acc[c, KEPT[8], half] + jnp.where(wraps[1], r5, 0.0) + jnp.where(wraps[3], r7, 0.0)
            sb[c, 8, half] = s8.astype(BF16)
        rb_copy(c, 8, x_peer(2)).start()
        for half in range(2):
            r1, r2, r3 = got(c, 1, half), got(c, 2, half), got(c, 3, half)
            r5, r7 = got(c, 5, half), got(c, 7, half)
            s4 = acc[c, KEPT[4], half] + jnp.where(wraps[1], r1, r5) + jnp.where(wraps[3], r3, r7)
            sb[c, 4, half] = (s4 + jnp.where(wraps[2], r2, 0.0)).astype(BF16)
            s0 = acc[c, KEPT[0], half] + jnp.where(wraps[1], 0.0, r1) + jnp.where(wraps[2], 0.0, r2)
            acc[c, KEPT[0], half] = s0 + jnp.where(wraps[3], 0.0, r3)
        rb_copy(c, 4, x_peer(3)).start()

    def last(c):
        came(c, 4)
        came(c, 8)
        cols = pl.ds(pl.multiple_of(c * HD, HD), HD)
        for half, result in ((0, dk_ref), (1, dv_ref)):
            total = acc[c, KEPT[0], half] + got(c, 4, half) + got(c, 8, half)
            result[:, cols] = total.astype(BF16)

    def rounds(i, carry):
        @pl.when(i < NKV)
        def _():
            backward(i)

        @pl.when((i >= 1) & (i < NKV + 1))
        def _():
            second(i - 1)

        @pl.when((i >= 2) & (i < NKV + 2))
        def _():
            third(i - 2)

        @pl.when(i >= 3)
        def _():
            last(i - 3)

        return carry

    lax.fori_loop(0, 2, rounds, 0)
    for step in range(1, SEQ):
        g_copy(step).wait_recv()
    gsum = g1[0]
    for block in range(1, SEQ):
        gsum = gsum + g1[block]
    gx[...] = gsum
    g2[my_dp] = gsum
    for step in range(1, DP):
        h_copy(step).start()
    lax.fori_loop(2, NKV + 3, rounds, 0)
    for step in range(1, DP):
        h_copy(step).wait_recv()
    gtot = g2[0]
    for block in range(1, DP):
        gtot = gtot + g2[block]
    at = lax.broadcasted_iota(jnp.int32, (8, HD), 1)
    grad = jnp.zeros((8, HD), F32)
    for column in range(HD // DP):
        one = jnp.sum(jnp.where(at == my_dp * (HD // DP) + column, gtot, 0.0), axis=1, keepdims=True)
        grad = jnp.where(at == column, one, grad)
    gr_ref[...] = grad[0 : NH // SEQ, 0 : HD // DP]

    def drain(c, carry):
        for number in range(9):
            kv_copy(c, 0, 0, 0, number).wait_send()
        for slot in range(1, NS):
            rb_copy(c, slot, 0).wait_send()
        return carry

    lax.fori_loop(0, NKV, drain, 0)
    for step in range(1, SEQ):
        og_copy(step).wait_send()
        g_copy(step).wait_send()
    for step in range(1, DP):
        h_copy(step).wait_send()


def on_device(
    queries, key_heads, value_heads, upper, readout, base, old, returns, source, lengths
):
    vmem = pl.BlockSpec(memory_space=pltpu.VMEM)
    dma = pltpu.SemaphoreType.DMA
    row = (1, T)
    outs = pl.pallas_call(
        kernel,
        name="critic",
        out_shape=(
            jax.ShapeDtypeStruct(row, F32),
            jax.ShapeDtypeStruct((T, NH * HD), BF16),
            jax.ShapeDtypeStruct((T, NKV * HD), BF16),
            jax.ShapeDtypeStruct((T, NKV * HD), BF16),
            jax.ShapeDtypeStruct((NH // SEQ, HD // DP), F32),
        ),
        in_specs=[vmem] * 9 + [pl.BlockSpec(memory_space=pltpu.SMEM)],
        out_specs=(vmem,) * 5,
        scratch_shapes=[
            pltpu.VMEM((NKV, 2, NS * T, HD), BF16),
            pltpu.VMEM((NKV, ROWS, NS * T), BF16),
            pltpu.VMEM((ROWS, NS * T), F32),
            pltpu.VMEM((T, NH * HD), BF16),
            pltpu.VMEM((ROWS, HD), BF16),
            pltpu.VMEM((NKV, ROWS, HD), F32),
            pltpu.VMEM((ROWS, HD), F32),
            pltpu.VMEM((T, NS * T), F32),
            pltpu.VMEM((T, HD), F32),
            pltpu.VMEM((T, HD), F32),
            pltpu.VMEM((NH, HD), F32),
            pltpu.VMEM((SEQ, 8, T), F32),
            pltpu.VMEM((NKV, NS, 2, T, HD), BF16),
            pltpu.VMEM((NKV, NS, 2, T, HD), BF16),
            pltpu.VMEM((NKV, 4, 2, T, HD), F32),
            pltpu.VMEM((SEQ, 8, HD), F32),
            pltpu.VMEM((SEQ, 8, HD), F32),
            pltpu.VMEM((DP, 8, HD), F32),
            pltpu.VMEM((8, HD), F32),
            pltpu.VMEM((NKV, 2, T, HD), BF16),
            dma((NKV, 9)), dma((NKV, NS)), dma((NKV,)), dma((SEQ,)), dma((SEQ,)), dma((NKV, NS)), dma((NKV, NS)),
            dma((SEQ,)), dma((SEQ,)), dma((DP,)), dma((DP,)),
        ],
        compiler_params=pltpu.CompilerParams(
            collective_id=0, has_side_effects=True, vmem_limit_bytes=60 * 1024 * 1024
        ),
    )(
        queries, key_heads, value_heads, upper, readout, base.reshape(row), old.reshape(row),
        returns.reshape(row), source.reshape(SEQ, T), lengths,
    )
    return (outs[0].reshape(T), *outs[1:])


def solution(mesh):
    tokens = P(("dp", "seq"))
    rows = P(("dp", "seq"), None)
    return jax.shard_map(
        on_device,
        mesh=mesh,
        in_specs=(rows, rows, rows, rows, P(), tokens, tokens, tokens, P("dp", None), P("dp", None)),
        out_specs=(tokens, rows, rows, rows, P("seq", "dp")),
        check_vma=False,
    )
```

```python
import jax
import jax.numpy as jnp
from jax import lax
from jax.experimental import pallas as pl
from jax.experimental.pallas import tpu as pltpu
from jax.sharding import PartitionSpec as P

T = 128
HD = 128
NH = 32
GROUP = 8
NKV = 4
SEQ = 16
DP = 16
NS = 9
ROWS = GROUP * T
CHUNKS = ((0, 256), (256, 512), (512, 768), (768, 1024), (1024, 1152))
KEPT = {0: 0, 2: 1, 4: 2, 8: 3}
SCALE = HD ** (-0.5)
LOG2E = 1.4426950408889634
MESH = pl.DeviceIdType.MESH
F32 = jnp.float32
BF16 = jnp.bfloat16
NT = (((1,), (1,)), ((), ()))
TN = (((0,), (0,)), ((), ()))


def dot(a, b, dims=(((1,), (0,)), ((), ()))):
    return lax.dot_general(a, b, dims, preferred_element_type=F32)


def heads_of(ref, first, count):
    wide = ref[:, pl.ds(pl.multiple_of(first * HD, HD), count * HD)]
    return jnp.concatenate([wide[:, a * HD : (a + 1) * HD] for a in range(count)], axis=0)


def kernel(
    q_hbm, k_ref, v_ref, u_hbm, ro_ref, base_ref, old_ref, ret_ref, src_ref, len_ref,
    vals_ref, dq_hbm, dk_ref, dv_ref, gr_ref,
    kv, p_sc, t_sc, out_sc, dol_sc, rl_sc, dl_sc, bias, vacc, cot_sc, ro, og, sb, rb, acc, gs, g1, g2, gx, tmp, q_ref, u_ref, dq_ref,
    kv_send, kv_recv, tmp_recv, og_send, og_recv, sb_send, rb_recv, g_send, g_recv, h_send, h_recv, in_sem, dq_sem,
):
    me = lax.axis_index("seq")
    my_dp = lax.axis_index("dp")
    x, y = me // 4, lax.rem(me, 4)

    def seq_peer(number):
        return {"seq": number}

    def row_peer(step):
        return x * 4 + lax.rem(y + step, 4)

    def x_peer(step):
        return lax.rem(x + step, 4) * 4 + y

    def send(src, dst, send_sem, recv_sem, peer):
        return pltpu.make_async_remote_copy(
            src_ref=src, dst_ref=dst, send_sem=send_sem, recv_sem=recv_sem, device_id=peer, device_id_type=MESH
        )

    def kv_copy(src, dst, half, peer, number):
        return send(
            kv.at[src, half], kv.at[dst, half], kv_send.at[number, half], kv_recv.at[dst, half], seq_peer(peer)
        )

    q_load = pltpu.make_async_copy(q_hbm, q_ref, in_sem.at[0])
    u_load = pltpu.make_async_copy(u_hbm, u_ref, in_sem.at[1])
    q_load.start()
    u_load.start()

    barrier = pltpu.get_barrier_semaphore()
    for step in range(1, SEQ):
        pl.semaphore_signal(
            barrier, inc=1, device_id={"seq": lax.rem(me + step, SEQ)}, device_id_type=MESH
        )
    for step in range(1, DP):
        pl.semaphore_signal(
            barrier, inc=1, device_id={"dp": lax.rem(my_dp + step, DP)}, device_id_type=MESH
        )

    ro[...] = ro_ref[...].astype(F32)
    for c in range(NKV):
        kv[c, 0, 0:T, :] = k_ref[:, c * HD : (c + 1) * HD]
        kv[c, 1, 0:T, :] = v_ref[:, c * HD : (c + 1) * HD]
    og[me] = jnp.concatenate([old_ref[...], ret_ref[...], jnp.zeros((6, T), F32)], axis=0)

    wraps = [y + step >= 4 for step in range(4)]
    lifts = [4 * (y + step >= 4).astype(jnp.int32) for step in range(4)]

    def piece(c, slot):
        return kv.at[c, :, pl.ds(pl.multiple_of(slot * T, T), T), :]

    def kv_copy(c, src, dst, peer, number):
        return send(
            piece(c, src), piece(c, dst), kv_send.at[c, number], kv_recv.at[c, dst], seq_peer(peer)
        )

    def landed(c, slot):
        kv_copy(c, 0, slot, 0, 0).wait_recv()

    pl.semaphore_wait(barrier, SEQ + DP - 2)

    def tmp_copy(c):
        return send(piece(c, 0), tmp.at[c], kv_send.at[c, 1], tmp_recv.at[c], seq_peer(x_peer(3)))

    def tmp_forward(c):
        return send(
            tmp.at[c], piece(c, 8), kv_send.at[c, 8], kv_recv.at[c, 8], seq_peer(x_peer(3))
        )

    def gather_start(c):
        kv_copy(c, 0, 4, x_peer(1), 0).start()
        tmp_copy(c).start()
        for step in range(1, 4):

            @pl.when(jnp.logical_not(wraps[step]))
            def _():
                kv_copy(c, 0, step, row_peer(step), 1 + step).start()

    def gather_forward(c):
        landed(c, 4)
        for step in (1, 3, 2):

            @pl.when(wraps[step])
            def _():
                kv_copy(c, 4, step, row_peer(step), 1 + step).start()

            if step != 2:

                @pl.when(jnp.logical_not(wraps[step]))
                def _():
                    kv_copy(c, 4, step + 4, row_peer(step), 4 + step).start()

        tmp_copy(c).wait_recv()
        tmp_forward(c).start()

    def gather_more(c):
        landed(c, 2)
        kv_copy(c, 2, 6, x_peer(1), 6).start()
        landed(c, 8)
        for step in (1, 3):

            @pl.when(wraps[step])
            def _():
                kv_copy(c, 8, step + 4, row_peer(step), 4 + step).start()

    gather_start(0)
    gather_start(1)

    def og_copy(step):
        return send(
            og.at[me], og.at[me], og_send.at[step], og_recv.at[step], seq_peer(lax.rem(me + step, SEQ))
        )

    for step in range(1, SEQ):
        og_copy(step).start()

    own_first = me * T
    place = own_first + lax.broadcasted_iota(jnp.int32, (T, 1), 0)
    c1 = len_ref[0, 0]
    c2 = c1 + len_ref[0, 1]
    c3 = c2 + len_ref[0, 2]
    first = jnp.where(place >= c3, c3, jnp.where(place >= c2, c2, jnp.where(place >= c1, c1, 0)))
    lane = lax.broadcasted_iota(jnp.int32, (1, T), 1)
    for slot in range(NS):
        key_place = own_first - T * slot + lane
        seen = (key_place >= first) & (key_place <= place)
        bias[:, slot * T : (slot + 1) * T] = jnp.where(seen, 0.0, -1e30)
    sub = lax.broadcasted_iota(jnp.int32, (T, T), 0)
    lanes = lax.broadcasted_iota(jnp.int32, (T, T), 1)
    own_src = src_ref[pl.ds(me, 1), :].astype(F32)
    columns = jnp.where(sub == 0, base_ref[...], jnp.where(sub == 1, own_src, 0.0)).T
    base_col = columns[:, 0:1]
    src_col = columns[:, 1:2]

    q_load.wait()
    u_load.wait()

    vacc[...] = jnp.zeros_like(vacc)
    gather_forward(0)
    gather_start(2)
    gather_forward(1)
    gather_more(0)
    gather_start(3)

    def forward(c, carry):
        @pl.when(c == 0)
        def _():
            gather_forward(2)
            gather_more(1)

        @pl.when(c == 1)
        def _():
            gather_forward(3)
            gather_more(2)

        @pl.when(c == 2)
        def _():
            gather_more(3)


        for slot in (1, 3, 5, 7, 6):
            landed(c, slot)
        h0 = c * GROUP
        q = heads_of(q_ref, h0, GROUP)
        top = None
        for low, high in CHUNKS:
            s = dot(q, kv[c, 0, low:high, :], NT)
            s = s.reshape(GROUP, T, high - low) * (SCALE * LOG2E) + bias[:, low:high][None]
            s = s.reshape(ROWS, high - low)
            t_sc[:, low:high] = s
            for at in range(0, high - low, T):
                part = s[:, at : at + T]
                top = part if top is None else jnp.maximum(top, part)
        top = jnp.max(top, axis=1, keepdims=True)
        total = None
        o = None
        for low, high in CHUNKS:
            e = jnp.exp2(t_sc[:, low:high] - top)
            for at in range(0, high - low, T):
                part = e[:, at : at + T]
                total = part if total is None else total + part
            e = e.astype(BF16)
            p_sc[c, :, low:high] = e
            part = dot(e, kv[c, 1, low:high, :])
            o = part if o is None else o + part
        rl = 1.0 / jnp.sum(total, axis=1, keepdims=True)
        rl_sc[c] = jnp.broadcast_to(rl, (ROWS, HD))
        o = (o * rl).astype(BF16)
        summed = vacc[...]
        for a in range(GROUP):
            one = o[a * T : (a + 1) * T]
            out_sc[:, pl.ds(pl.multiple_of((h0 + a) * HD, HD), HD)] = one
            summed = summed + one.astype(F32) * ro[pl.ds(h0 + a, 1), :]
        vacc[...] = summed
        return carry

    lax.fori_loop(0, 2, forward, 0)

    for step in range(1, SEQ):
        og_copy(step).wait_recv()
    old_acc = jnp.zeros((T, T), F32)
    ret_acc = jnp.zeros((T, T), F32)
    for block in range(SEQ):
        same = src_col == (lane + block * T).astype(F32)
        old_acc = old_acc + jnp.where(same, og[block, 0:1, :], 0.0)
        ret_acc = ret_acc + jnp.where(same, og[block, 1:2, :], 0.0)
    old_now = jnp.sum(old_acc, axis=1, keepdims=True)
    return_now = jnp.sum(ret_acc, axis=1, keepdims=True)
    lax.fori_loop(2, NKV, forward, 0)

    values = base_col + jnp.sum(vacc[...], axis=1, keepdims=True)
    vals_ref[...] = jnp.where(lanes == 0, values, 0.0).T[0:1, :]
    ratio = jnp.tanh((values - old_now) / 0.2)
    plain = values - return_now
    gap = old_now + 0.2 * ratio - return_now
    mixing = jax.nn.sigmoid((plain * plain - gap * gap) / 0.1)
    cot = 16.0 * (mixing * plain + (1.0 - mixing) * gap * (1.0 - ratio * ratio))
    cot_sc[...] = jnp.broadcast_to(cot, (T, HD))

    def g_copy(step):
        peer = lax.rem(me + step, SEQ)
        return send(gs.at[peer], g1.at[me], g_send.at[step], g_recv.at[step], seq_peer(peer))

    def h_copy(step):
        peer = lax.rem(my_dp + step, DP)
        return send(gx, g2.at[my_dp], h_send.at[step], h_recv.at[step], {"dp": peer})

    def rb_copy(c, slot, peer):
        return send(
            sb.at[c, slot], rb.at[c, slot], sb_send.at[c, slot], rb_recv.at[c, slot], seq_peer(peer)
        )

    def came(c, slot):
        rb_copy(c, slot, 0).wait_recv()

    def got(c, slot, half):
        return rb[c, slot, half].astype(F32)

    def dq_store(c):
        cols = pl.ds(pl.multiple_of(c * ROWS, ROWS), ROWS)
        return pltpu.make_async_copy(dq_ref.at[:, cols], dq_hbm.at[:, cols], dq_sem.at[c])

    def backward(c):
        h0 = c * GROUP
        cot = cot_sc[...]
        q = heads_of(q_ref, h0, GROUP)
        dols = []
        dls = []
        for a in range(GROUP):
            cols = pl.ds(pl.multiple_of((h0 + a) * HD, HD), HD)
            row = pl.ds(h0 + a, 1)
            o = out_sc[:, cols].astype(F32)
            g = (u_ref[:, cols].astype(F32) + cot * ro[row, :]).astype(BF16).astype(F32)
            rl = rl_sc[c, a * T : (a + 1) * T, :]
            dls.append(jnp.broadcast_to(jnp.sum(g * o, axis=1, keepdims=True), (T, HD)) * rl)
            dols.append((g * rl).astype(BF16))
        dol = jnp.concatenate(dols, axis=0)
        dl_sc[...] = jnp.concatenate(dls, axis=0)
        dol_sc[...] = dol
        qt = jnp.concatenate([q[a * T : (a + 1) * T].T for a in range(GROUP)], axis=1)
        dolt = jnp.concatenate([dols[a].T for a in range(GROUP)], axis=1)
        dq = None
        for first_slot in (6, 4, 0, 2, 8):
            low, high = first_slot * T, min(first_slot + 2, NS) * T
            dol = dol_sc[...]
            keys = kv[c, 0, low:high, :]
            dl = dl_sc[...]
            if high - low > T:
                dl = jnp.concatenate([dl] * ((high - low) // T), axis=1)
            p = p_sc[c, :, low:high]
            ds = (p.astype(F32) * (dot(dol, kv[c, 1, low:high, :], NT) - dl)).astype(BF16)
            part = dot(ds, keys)
            dq = part if dq is None else dq + part
            dk = dot(qt, ds) * SCALE
            dv = dot(dolt, p)
            for at in range(0, high - low, T):
                slot = (low + at) // T
                if slot in KEPT:
                    acc[c, KEPT[slot], 0] = dk[:, at : at + T]
                    acc[c, KEPT[slot], 1] = dv[:, at : at + T]
                else:
                    sb[c, slot, 0] = dk[:, at : at + T].astype(BF16)
                    sb[c, slot, 1] = dv[:, at : at + T].astype(BF16)
                    if slot == 6:
                        rb_copy(c, 6, x_peer(3)).start()
                    else:
                        rb_copy(c, slot, row_peer(4 - slot % 4)).start()
        dq = (dq * SCALE).astype(BF16)
        for a in range(GROUP):
            dq_ref[:, pl.ds(pl.multiple_of((h0 + a) * HD, HD), HD)] = dq[a * T : (a + 1) * T]
        dq_store(c).start()

    def second(c):
        came(c, 6)
        for half in range(2):
            sb[c, 2, half] = (acc[c, KEPT[2], half] + got(c, 6, half)).astype(BF16)
        rb_copy(c, 2, row_peer(2)).start()

    def third(c):
        for slot in (5, 7, 1, 3, 2):
            came(c, slot)
        for half in range(2):
            r5, r7 = got(c, 5, half), got(c, 7, half)
            s8 = acc[c, KEPT[8], half] + jnp.where(wraps[1], r5, 0.0) + jnp.where(wraps[3], r7, 0.0)
            sb[c, 8, half] = s8.astype(BF16)
        rb_copy(c, 8, x_peer(2)).start()
        for half in range(2):
            r1, r2, r3 = got(c, 1, half), got(c, 2, half), got(c, 3, half)
            r5, r7 = got(c, 5, half), got(c, 7, half)
            s4 = acc[c, KEPT[4], half] + jnp.where(wraps[1], r1, r5) + jnp.where(wraps[3], r3, r7)
            s4 = s4 + jnp.where(wraps[2], r2, 0.0)
            sb[c, 4, half] = s4.astype(BF16)
        rb_copy(c, 4, x_peer(3)).start()
        for half in range(2):
            r1, r2, r3 = got(c, 1, half), got(c, 2, half), got(c, 3, half)
            s0 = acc[c, KEPT[0], half] + jnp.where(wraps[1], 0.0, r1) + jnp.where(wraps[2], 0.0, r2)
            acc[c, KEPT[0], half] = s0 + jnp.where(wraps[3], 0.0, r3)

    def last(c):
        came(c, 4)
        came(c, 8)
        cols = pl.ds(pl.multiple_of(c * HD, HD), HD)
        for half, result in ((0, dk_ref), (1, dv_ref)):
            total = acc[c, KEPT[0], half] + got(c, 4, half) + got(c, 8, half)
            result[:, cols] = total.T.astype(BF16)

    def rounds(i, carry):
        @pl.when(i < NKV)
        def _():
            backward(i)

        @pl.when(i < NKV + 1)
        def _():
            second(i - 1)

        @pl.when((i >= 2) & (i < NKV + 2))
        def _():
            third(i - 2)

        @pl.when(i >= 3)
        def _():
            last(i - 3)

        return carry

    backward(0)
    wide_cot = cot_sc[...]
    for h in range(NH):
        o = out_sc[:, h * HD : (h + 1) * HD].astype(F32)
        gs[h // 2, h % 2 : h % 2 + 1, :] = jnp.sum(wide_cot * o, axis=0, keepdims=True)
    g1[me] = gs[me]
    for step in range(1, SEQ):
        g_copy(step).start()

    lax.fori_loop(1, 2, rounds, 0)

    for step in range(1, SEQ):
        g_copy(step).wait_recv()
    gsum = g1[0]
    for block in range(1, SEQ):
        gsum = gsum + g1[block]
    gx[...] = gsum
    g2[my_dp] = gsum
    for step in range(1, DP):
        h_copy(step).start()
    lax.fori_loop(2, NKV + 3, rounds, 0)
    for step in range(1, DP):
        h_copy(step).wait_recv()
    gtot = g2[0]
    for block in range(1, DP):
        gtot = gtot + g2[block]
    at = lax.broadcasted_iota(jnp.int32, (8, HD), 1)
    grad = jnp.zeros((8, HD), F32)
    for column in range(HD // DP):
        one = jnp.sum(jnp.where(at == my_dp * (HD // DP) + column, gtot, 0.0), axis=1, keepdims=True)
        grad = jnp.where(at == column, one, grad)
    gr_ref[...] = grad[0 : NH // SEQ, 0 : HD // DP]

    def drain(c, carry):
        dq_store(c).wait()
        for number in range(9):
            kv_copy(c, 0, 0, 0, number).wait_send()
        for slot in range(1, NS):
            rb_copy(c, slot, 0).wait_send()
        return carry

    lax.fori_loop(0, NKV, drain, 0)
    for step in range(1, SEQ):
        og_copy(step).wait_send()
        g_copy(step).wait_send()
    for step in range(1, DP):
        h_copy(step).wait_send()


def store_results(*refs):
    sems = refs[-1]
    pieces = []
    for i in range(5):
        src, dst, hold = refs[i], refs[5 + i], refs[10 + i]
        if i == 1:
            for at in range(0, T, T // 4):
                rows = pl.ds(at, T // 4)
                pieces.append((src.at[rows, :], hold.at[rows, :], dst.at[rows, :]))
        else:
            pieces.append((src, hold, dst))
    loads = [pltpu.make_async_copy(a, b, sems.at[0, n]) for n, (a, b, _) in enumerate(pieces)]
    stores = [pltpu.make_async_copy(b, c, sems.at[1, n]) for n, (_, b, c) in enumerate(pieces)]
    for copy in loads:
        copy.start()
    for load, store in zip(loads, stores):
        load.wait()
        store.start()
    for copy in stores:
        copy.wait()


def on_device(
    queries, key_heads, value_heads, upper, readout, base, old, returns, source, lengths
):
    vmem = pl.BlockSpec(memory_space=pltpu.VMEM)
    anywhere = pl.BlockSpec(memory_space=pl.ANY)
    dma = pltpu.SemaphoreType.DMA
    row = (1, T)
    outs = pl.pallas_call(
        kernel,
        name="critic",
        out_shape=(
            jax.ShapeDtypeStruct(row, F32),
            jax.ShapeDtypeStruct((T, NH * HD), BF16),
            jax.ShapeDtypeStruct((T, NKV * HD), BF16),
            jax.ShapeDtypeStruct((T, NKV * HD), BF16),
            jax.ShapeDtypeStruct((NH // SEQ, HD // DP), F32),
        ),
        in_specs=[anywhere, vmem, vmem, anywhere] + [vmem] * 5 + [pl.BlockSpec(memory_space=pltpu.SMEM)],
        out_specs=(vmem, anywhere, vmem, vmem, vmem),
        scratch_shapes=[
            pltpu.VMEM((NKV, 2, NS * T, HD), BF16),
            pltpu.VMEM((NKV, ROWS, NS * T), BF16),
            pltpu.VMEM((ROWS, NS * T), F32),
            pltpu.VMEM((T, NH * HD), BF16),
            pltpu.VMEM((ROWS, HD), BF16),
            pltpu.VMEM((NKV, ROWS, HD), F32),
            pltpu.VMEM((ROWS, HD), F32),
            pltpu.VMEM((T, NS * T), F32),
            pltpu.VMEM((T, HD), F32),
            pltpu.VMEM((T, HD), F32),
            pltpu.VMEM((NH, HD), F32),
            pltpu.VMEM((SEQ, 8, T), F32),
            pltpu.VMEM((NKV, NS, 2, T, HD), BF16),
            pltpu.VMEM((NKV, NS, 2, T, HD), BF16),
            pltpu.VMEM((NKV, 4, 2, T, HD), F32),
            pltpu.VMEM((SEQ, 8, HD), F32),
            pltpu.VMEM((SEQ, 8, HD), F32),
            pltpu.VMEM((DP, 8, HD), F32),
            pltpu.VMEM((8, HD), F32),
            pltpu.VMEM((NKV, 2, T, HD), BF16),
            pltpu.VMEM((T, NH * HD), BF16),
            pltpu.VMEM((T, NH * HD), BF16),
            pltpu.VMEM((T, NH * HD), BF16),
            dma((NKV, 9)), dma((NKV, NS)), dma((NKV,)), dma((SEQ,)), dma((SEQ,)), dma((NKV, NS)), dma((NKV, NS)),
            dma((SEQ,)), dma((SEQ,)), dma((DP,)), dma((DP,)), dma((2,)), dma((NKV,)),
        ],
        compiler_params=pltpu.CompilerParams(
            collective_id=0, has_side_effects=True, vmem_limit_bytes=60 * 1024 * 1024
        ),
    )(
        queries, key_heads, value_heads, upper, readout, base.reshape(row), old.reshape(row),
        returns.reshape(row), source.reshape(SEQ, T), lengths,
    )
    outs = pl.pallas_call(
        store_results,
        name="store",
        out_shape=tuple(jax.ShapeDtypeStruct(out.shape, out.dtype) for out in outs),
        in_specs=[anywhere] * 5,
        out_specs=(anywhere,) * 5,
        scratch_shapes=[pltpu.VMEM(out.shape, out.dtype) for out in outs] + [dma((2, 8))],
    )(*outs)
    return (outs[0].reshape(T), *outs[1:])


def solution(mesh):
    tokens = P(("dp", "seq"))
    rows = P(("dp", "seq"), None)
    return jax.shard_map(
        on_device,
        mesh=mesh,
        in_specs=(rows, rows, rows, rows, P(), tokens, tokens, tokens, P("dp", None), P("dp", None)),
        out_specs=(tokens, rows, rows, rows, P("seq", "dp")),
        check_vma=False,
    )
```
